512 devices in a mesh: ctx: 64 (over x, z), tp: 8 (over y, core).
Axes of the slice: x: 4, y: 4, z: 16, core: 2. Of those that a mesh axis runs over, the one named last changes fastest.
Arguments:
- queries: bfloat16 [16384, 128, 128], P('ctx', 'tp'), may hold values from -80 to 80
- keys: bfloat16 [16384, 8, 128], P(('ctx', 'tp')), may hold values from -4 to 4
- values: bfloat16 [16384, 8, 128], P(('ctx', 'tp')), may hold values from -6 to 6
- output_gradient: bfloat16 [16384, 128, 128], P('ctx', 'tp'), may hold values from -6 to 6
- doc_blocks: int32 [64], replicated, may hold values from 1 to 5, 128 in all
Outputs:
- query_grads: bfloat16 [16384, 128, 128], P('ctx', 'tp')
- key_gradient: bfloat16 [16384, 8, 128], P(('ctx', 'tp'))
- value_gradient: bfloat16 [16384, 8, 128], P(('ctx', 'tp'))
The draws below stay inside these ranges and needn't reach their ends.
Inputs may be any that keep to these rules, and one draw needn't show every extreme that they name: `doc_blocks`: document lengths in blocks of 128 tokens; they sum to 128 and the longest has exactly 5 blocks.
All inputs are finite; a program needn't handle non-finite values.
Results may differ from the reference program's by a relative error of at most 0.0082.
Values may be sent and summed in bfloat16 or wider, within the bound.
No kernel may reach another device: no remote copies, remote signals or barrier semaphores. Data moves between devices by JAX's collectives and lax.ppermute only.
A program may use at most 128 MiB of HBM per device.

```python
import math
import jax
import jax.numpy as jnp
import numpy as np
from jax import lax

QUERY_HEADS = 128
KEY_VALUE_HEADS = 8
HEAD_DIM = 128
BLK = 128
PACKED_TOKENS = 16384
NBLK = 128
MOSTB = 5
NDOCS = 64


def common_keys(key):
    base_offset = jax.random.normal(jax.random.fold_in(key, 11), (PACKED_TOKENS, KEY_VALUE_HEADS, HEAD_DIM), jnp.float32)
    return jnp.clip(base_offset, -4.0, 4.0)


def draw_keys(key, part):
    base_offset = common_keys(key)
    return base_offset.astype(jnp.bfloat16)


def draw_queries(key, part):
    fresh = jax.random.normal(jax.random.fold_in(key, 12), (PACKED_TOKENS, QUERY_HEADS, HEAD_DIM), jnp.float32)
    fresh = jnp.clip(fresh, -6.0, 6.0)
    return fresh.astype(jnp.bfloat16)


def block_levels(rng, shape, split, least, top_value):
    def one(axis_at, blocks):
        heights = jax.random.uniform(jax.random.fold_in(jax.random.fold_in(rng, 6), axis_at), (blocks,), jnp.float32, least / len(split), top_value / len(split))
        return jnp.repeat(jnp.exp(heights), shape[axis_at] // blocks).reshape((-1,) + (1,) * (len(shape) - axis_at - 1))

    gain = one(*split[0])
    for cut in split[1:]:
        gain = gain * one(*cut)
    return gain


def split_up(amount, total, limit, skew):
    portions = [(1 << 20) // math.isqrt(standing ** skew) + 1 for standing in range(2, amount + 1)]
    surplus, holding = total - limit - (amount - 1), [1] * (amount - 1)
    while surplus > 0:
        candidates = [i for i in range(amount - 1) if holding[i] < limit]
        mass, budget = sum([portions[i] for i in candidates]), surplus
        for i in candidates:
            more = min(limit - holding[i], max(1, budget * portions[i] // mass), surplus)
            holding[i] = holding[i] + more
            surplus = surplus - more
    return np.array([limit] + holding)


def ragged(own_key, count, total, bound, skew):
    if count == 2:
        one = jax.random.randint(own_key, (), max(1, total - bound), min(bound, total - 1) + 1)
        return jnp.stack([one, total - one])
    lengths = jnp.asarray(split_up(count, total, bound, skew), jnp.int32)
    pairs = (count - 1) // 2
    source_of, taker = lengths[1:1 + 2 * pairs:2], lengths[2:2 + 2 * pairs:2]
    margin = jnp.minimum(source_of - 1, bound - taker)
    moved = jax.random.randint(jax.random.fold_in(own_key, 1), (pairs,), 0, 1 << 20) % (margin + 1)
    lengths = lengths.at[1:1 + 2 * pairs:2].set(source_of - moved).at[2:2 + 2 * pairs:2].set(taker + moved)
    return lengths[jax.random.permutation(jax.random.fold_in(own_key, 2), count)]


def normal_values(key, shape, scale, reach, cuts=(), kind=jnp.bfloat16):
    drawn = scale * jax.random.normal(key, shape, jnp.float32)
    if cuts:
        drawn = drawn * block_levels(key, shape, cuts, -0.22, 0.18)
    return jnp.clip(drawn, -reach, reach).astype(kind)


def setup_inputs(seed: int = 0) -> dict:
    seeds = jax.random.split(jax.random.key(seed), 6)
    return {
        "queries": draw_queries(jax.random.fold_in(seeds[5], 71), 0),
        "keys": draw_keys(jax.random.fold_in(seeds[5], 71), 0),
        "values": normal_values(seeds[2], (PACKED_TOKENS, KEY_VALUE_HEADS, HEAD_DIM), 1.0, 6.0, ((0, 512),)),
        "output_gradient": normal_values(seeds[3], (PACKED_TOKENS, QUERY_HEADS, HEAD_DIM), 1.0, 6.0, ((0, 64), (1, 8))),
        "doc_blocks": ragged(seeds[4], NDOCS, NBLK, MOSTB, 1).astype(jnp.int32),
    }


def rounded(array):
    return lax.optimization_barrier(array.astype(jnp.bfloat16)).astype(jnp.float32)

def token_docs(doc_blocks):
    ends = jnp.cumsum(doc_blocks).astype(jnp.int32)
    blocks = jnp.arange(NBLK, dtype=jnp.int32)
    block_doc = lax.optimization_barrier(jnp.sum((ends[None, :] <= blocks[:, None]).astype(jnp.int32), axis=1))
    return jnp.repeat(block_doc, BLK)

def reference(queries, keys, values, output_gradient, doc_blocks):
    group_ratio = QUERY_HEADS // KEY_VALUE_HEADS
    scale = 1.0 / math.sqrt(HEAD_DIM)
    width = MOSTB * BLK
    docs = token_docs(doc_blocks)
    positions = jnp.arange(PACKED_TOKENS, dtype=jnp.int32)
    query_full = queries.astype(jnp.float32).reshape(PACKED_TOKENS, KEY_VALUE_HEADS, group_ratio, HEAD_DIM)
    gradient_full = output_gradient.astype(jnp.float32).reshape(PACKED_TOKENS, KEY_VALUE_HEADS, group_ratio, HEAD_DIM)
    key_all = keys.astype(jnp.float32)
    value_all = values.astype(jnp.float32)

    def query_block(block):
        start = (block * BLK).astype(jnp.int32)
        key_start = jnp.maximum(start - (MOSTB - 1) * BLK, 0).astype(jnp.int32)
        query_rows = lax.dynamic_slice_in_dim(query_full, start, BLK, 0)
        grad_rows = lax.dynamic_slice_in_dim(gradient_full, start, BLK, 0)
        key_rows = lax.dynamic_slice_in_dim(key_all, key_start, width, 0)
        value_rows = lax.dynamic_slice_in_dim(value_all, key_start, width, 0)
        query_pos = lax.dynamic_slice_in_dim(positions, start, BLK, 0)
        key_pos = lax.dynamic_slice_in_dim(positions, key_start, width, 0)
        query_doc = lax.dynamic_slice_in_dim(docs, start, BLK, 0)
        key_doc = lax.dynamic_slice_in_dim(docs, key_start, width, 0)
        allowed = (query_doc[:, None] == key_doc[None, :]) & (key_pos[None, :] <= query_pos[:, None])
        scores = jnp.einsum('qgrd,kgd->grqk', query_rows, key_rows) * scale
        scores = jnp.where(allowed, scores, -1e+30)
        top = lax.optimization_barrier(jnp.max(scores, axis=-1))
        total = lax.optimization_barrier(jnp.sum(jnp.exp(scores - top[..., None]), axis=-1))
        probs = jnp.exp(scores - top[..., None]) / total[..., None]
        output = jnp.einsum('grqk,kgd->qgrd', rounded(probs), value_rows)
        delta = jnp.einsum('qgrd,qgrd->grq', grad_rows, output)
        dprobs = jnp.einsum('qgrd,kgd->grqk', grad_rows, value_rows)
        dscores = rounded(probs * (dprobs - delta[..., None]) * scale)
        query_grad = jnp.einsum('grqk,kgd->qgrd', dscores, key_rows)
        return (query_grad.reshape(BLK, QUERY_HEADS, HEAD_DIM).astype(jnp.bfloat16), top, total, delta)
    query_parts, top_values, total_sums, delta_rows = lax.map(query_block, jnp.arange(NBLK, dtype=jnp.int32))
    query_grads = query_parts.reshape(PACKED_TOKENS, QUERY_HEADS, HEAD_DIM)
    top_values = jnp.transpose(top_values, (1, 2, 0, 3)).reshape(KEY_VALUE_HEADS, group_ratio, PACKED_TOKENS)
    total_sums = jnp.transpose(total_sums, (1, 2, 0, 3)).reshape(KEY_VALUE_HEADS, group_ratio, PACKED_TOKENS)
    delta_rows = jnp.transpose(delta_rows, (1, 2, 0, 3)).reshape(KEY_VALUE_HEADS, group_ratio, PACKED_TOKENS)

    def key_block(block):
        start = (block * BLK).astype(jnp.int32)
        query_start = jnp.minimum(start, PACKED_TOKENS - width).astype(jnp.int32)
        key_rows = lax.dynamic_slice_in_dim(key_all, start, BLK, 0)
        value_rows = lax.dynamic_slice_in_dim(value_all, start, BLK, 0)
        query_rows = lax.dynamic_slice_in_dim(query_full, query_start, width, 0)
        grad_rows = lax.dynamic_slice_in_dim(gradient_full, query_start, width, 0)
        top = lax.dynamic_slice_in_dim(top_values, query_start, width, 2)
        total = lax.dynamic_slice_in_dim(total_sums, query_start, width, 2)
        delta = lax.dynamic_slice_in_dim(delta_rows, query_start, width, 2)
        key_pos = lax.dynamic_slice_in_dim(positions, start, BLK, 0)
        query_pos = lax.dynamic_slice_in_dim(positions, query_start, width, 0)
        key_doc = lax.dynamic_slice_in_dim(docs, start, BLK, 0)
        query_doc = lax.dynamic_slice_in_dim(docs, query_start, width, 0)
        allowed = (query_doc[:, None] == key_doc[None, :]) & (key_pos[None, :] <= query_pos[:, None])
        scores = jnp.einsum('qgrd,kgd->grqk', query_rows, key_rows) * scale
        scores = jnp.where(allowed, scores, -1e+30)
        probs = jnp.exp(scores - top[..., None]) / total[..., None]
        dprobs = jnp.einsum('qgrd,kgd->grqk', grad_rows, value_rows)
        dscores = rounded(probs * (dprobs - delta[..., None]) * scale)
        key_grad = jnp.einsum('grqk,qgrd->kgd', dscores, query_rows)
        value_grad = jnp.einsum('grqk,qgrd->kgd', rounded(probs), grad_rows)
        return (key_grad.astype(jnp.bfloat16), value_grad.astype(jnp.bfloat16))
    key_pieces, value_pieces = lax.map(key_block, jnp.arange(NBLK, dtype=jnp.int32))
    key_gradient = key_pieces.reshape(PACKED_TOKENS, KEY_VALUE_HEADS, HEAD_DIM)
    value_gradient = value_pieces.reshape(PACKED_TOKENS, KEY_VALUE_HEADS, HEAD_DIM)
    return (query_grads, key_gradient, value_gradient)
```

```python
import functools
import math

import jax
import jax.numpy as jnp
from jax import lax
from jax.experimental import pallas as pl
from jax.experimental.pallas import tpu as pltpu
from jax.sharding import PartitionSpec as P

BLK = 128
BLK_DEV = 2
BACK = 4
LOG2E = math.log2(math.e)
LOW = -3.0e38
OFF = 1.0e30

VMEM = pl.BlockSpec(memory_space=pltpu.VMEM)
SMEM = pl.BlockSpec(memory_space=pltpu.SMEM)


def passed_along(block, axis, distance):
    devices = range(lax.axis_size(axis))
    route = [(i - distance, i) for i in devices if i - distance in devices]
    return lax.ppermute(block, axis, route)


def to_groups(k_ref, v_ref, out_ref, wide):
    for which, ref in enumerate((k_ref, v_ref)):
        wide[...] = ref[...].astype(jnp.float32)
        for g in range(wide.shape[1]):
            out_ref[g, which] = wide[:, g, :].astype(out_ref.dtype)


def from_groups(in_ref, k_ref, v_ref, wide):
    for which, ref in enumerate((k_ref, v_ref)):
        for g in range(wide.shape[1]):
            wide[:, g, :] = in_ref[g, which].astype(jnp.float32)
        ref[...] = wide[...].astype(ref.dtype)


def attention(prev_ref, q_ref, g_ref, x0_ref, x1_ref, x2_ref,
              dq_ref, y0_ref, y1_ref, y2_ref,
              kk, vv, kt, dk, dv, *, heads):
    step = pl.program_id(0)
    steps = pl.num_programs(0)
    head_size = q_ref.shape[1]
    rows = q_ref.shape[0]
    span = (BACK + 1) * BLK
    scale = 1.0 / math.sqrt(head_size)
    factor = scale * LOG2E
    local = BLK_DEV * BLK
    f32 = jnp.float32

    @pl.when(step == 0)
    def _():
        for i, ref in enumerate((x2_ref, x1_ref, x0_ref)):
            k = ref[:, 0].reshape(local, head_size)
            kk[pl.ds(i * local, local), :] = k
            vv[pl.ds(i * local, local), :] = ref[:, 1].reshape(local, head_size)
            kt[:, pl.ds(i * local, local)] = k.astype(f32).T.astype(kk.dtype)
        dk[...] = jnp.zeros_like(dk)
        dv[...] = jnp.zeros_like(dv)

    half = steps // BLK_DEV

    def work(block):
        base = block * BLK
        prev = prev_ref[block]
        window = pl.ds(base, span)
        q = q_ref[...]
        g = g_ref[...]
        nt = (((1,), (1,)), ((), ()))
        st = lax.dot_general(kk[window, :], q, nt, preferred_element_type=f32)
        dpt = lax.dot_general(vv[window, :], g, nt, preferred_element_type=f32)
        first_row = (step - block * half) * rows
        key = lax.broadcasted_iota(jnp.int32, (BLK, rows), 0) * heads
        row = lax.broadcasted_iota(jnp.int32, (BLK, rows), 1) + first_row
        parts = [st[o * BLK:(o + 1) * BLK] for o in range(BACK + 1)]
        parts[BACK] = jnp.where(key <= row, parts[BACK], -OFF)
        off = [jnp.where(prev >= BACK - o, 0.0, OFF).astype(f32) for o in range(BACK)] + [None]
        top = jnp.max(parts[BACK], axis=0, keepdims=True)
        for o in range(BACK):
            top = jnp.maximum(top, jnp.max(parts[o], axis=0, keepdims=True) - off[o])
        low = top * factor
        total = jnp.zeros((1, rows), f32)
        es = []
        for o in range(BACK + 1):
            shift = low if off[o] is None else low + off[o]
            e = jnp.exp2(parts[o] * factor - shift)
            total = total + jnp.sum(e, axis=0, keepdims=True)
            es.append(e)
        inv = 1.0 / total
        delta = jnp.zeros((1, rows), f32)
        fs, ps, ds = [], [], []
        for o in range(BACK + 1):
            p = es[o] * inv
            p_round = p.astype(kk.dtype)
            d = dpt[o * BLK:(o + 1) * BLK]
            delta = delta + jnp.sum(p_round.astype(f32) * d, axis=0, keepdims=True)
            fs.append(p)
            ps.append(p_round)
        for o in range(BACK + 1):
            d = dpt[o * BLK:(o + 1) * BLK]
            ds.append((fs[o] * (d - delta) * scale).astype(kk.dtype))
        p_low = jnp.concatenate(ps, axis=0)
        d_low = jnp.concatenate(ds, axis=0)
        dv[window, :] += jnp.dot(p_low, g, preferred_element_type=f32)
        dk[window, :] += jnp.dot(d_low, q, preferred_element_type=f32)
        dqt = jnp.dot(kt[:, window], d_low, preferred_element_type=f32)
        dq_ref[...] = dqt.T.astype(dq_ref.dtype)

    for block in range(BLK_DEV):
        pl.when(step // half == block)(functools.partial(work, block))

    @pl.when(step == steps - 1)
    def _():
        for i, ref in enumerate((y2_ref, y1_ref, y0_ref)):
            k = dk[pl.ds(i * local, local), :]
            v = dv[pl.ds(i * local, local), :]
            ref[:, 0] = k.astype(ref.dtype).reshape(ref.shape[0], -1, head_size)
            ref[:, 1] = v.astype(ref.dtype).reshape(ref.shape[0], -1, head_size)


def local_grads(prev, q, g, x0, x1, x2, heads, rows=512):
    total_rows, head_size = q.shape
    steps = total_rows // rows
    keys = 3 * BLK_DEV * BLK
    row_spec = pl.BlockSpec((rows, head_size), lambda i: (i, 0))
    low = q.dtype
    return pl.pallas_call(
        functools.partial(attention, heads=heads),
        grid=(steps,),
        out_shape=(
            jax.ShapeDtypeStruct(q.shape, low),
            jax.ShapeDtypeStruct(x0.shape, low),
            jax.ShapeDtypeStruct(x0.shape, low),
            jax.ShapeDtypeStruct(x0.shape, low),
        ),
        in_specs=[SMEM, row_spec, row_spec, VMEM, VMEM, VMEM],
        out_specs=(row_spec, VMEM, VMEM, VMEM),
        scratch_shapes=[
            pltpu.VMEM((keys, head_size), low),
            pltpu.VMEM((keys, head_size), low),
            pltpu.VMEM((head_size, keys), low),
            pltpu.VMEM((keys, head_size), jnp.float32),
            pltpu.VMEM((keys, head_size), jnp.float32),
        ],
        compiler_params=pltpu.CompilerParams(
            dimension_semantics=("arbitrary",), vmem_limit_bytes=48 << 20
        ),
        name="local_grads",
    )(prev, q, g, x0, x1, x2)


def on_device(queries, keys, values, output_gradient, doc_blocks):
    tok_count, heads, head_size = queries.shape
    tok_part, groups, _ = keys.shape
    low = queries.dtype
    packed = pl.pallas_call(
        to_groups,
        out_shape=jax.ShapeDtypeStruct((groups, 2, tok_part, head_size), low),
        in_specs=[VMEM, VMEM],
        out_specs=VMEM,
        scratch_shapes=[pltpu.VMEM(keys.shape, jnp.float32)],
        name="to_groups",
    )(keys, values)
    x0 = lax.all_to_all(packed, "tp", split_axis=0, concat_axis=0, tiled=True)
    x1 = passed_along(x0, "ctx", 1)
    x2 = passed_along(x0, "ctx", 2)
    docs = doc_blocks.shape[0]
    upto = jnp.arange(docs)[:, None] >= jnp.arange(docs)[None, :]
    ends = jnp.sum(jnp.where(upto, doc_blocks[None, :], 0), axis=1)
    mine = lax.axis_index("ctx") * BLK_DEV + jnp.arange(BLK_DEV, dtype=jnp.int32)
    start = jnp.max(jnp.where(ends[None, :] <= mine[:, None], ends[None, :], 0), axis=1)
    prev = (mine - start).astype(jnp.int32)
    dq, y0, y1, y2 = local_grads(
        prev,
        queries.reshape(tok_count * heads, head_size),
        output_gradient.reshape(tok_count * heads, head_size),
        x0, x1, x2, heads,
    )
    r2 = passed_along(y2, "ctx", -2)
    r1 = passed_along(y1, "ctx", -1)
    f32 = jnp.float32
    summed = (y0.astype(f32) + r1.astype(f32) + r2.astype(f32)).astype(low)
    back = lax.all_to_all(summed, "tp", split_axis=0, concat_axis=0, tiled=True)
    key_gradient, value_gradient = pl.pallas_call(
        from_groups,
        out_shape=(
            jax.ShapeDtypeStruct(keys.shape, low),
            jax.ShapeDtypeStruct(values.shape, low),
        ),
        in_specs=[VMEM],
        out_specs=(VMEM, VMEM),
        scratch_shapes=[pltpu.VMEM(keys.shape, jnp.float32)],
        name="from_groups",
    )(back)
    return dq.reshape(queries.shape), key_gradient, value_gradient


def solution(mesh):
    return jax.shard_map(
        on_device,
        mesh=mesh,
        in_specs=(
            P("ctx", "tp", None),
            P(("ctx", "tp"), None, None),
            P(("ctx", "tp"), None, None),
            P("ctx", "tp", None),
            P(),
        ),
        out_specs=(
            P("ctx", "tp", None),
            P(("ctx", "tp"), None, None),
            P(("ctx", "tp"), None, None),
        ),
        check_vma=False,
    )
```

```python
import functools
import math

import jax
import jax.numpy as jnp
from jax import lax
from jax.experimental import pallas as pl
from jax.experimental.pallas import tpu as pltpu
from jax.sharding import PartitionSpec as P

BLK = 128
BLK_DEV = 2
BACK = 4
LOG2E = math.log2(math.e)
LOW = -3.0e38
OFF = 1.0e30

VMEM = pl.BlockSpec(memory_space=pltpu.VMEM)
SMEM = pl.BlockSpec(memory_space=pltpu.SMEM)
HBM = pl.BlockSpec(memory_space=pltpu.HBM)


def passed_along(block, axis, distance):
    devices = range(lax.axis_size(axis))
    route = [(i - distance, i) for i in devices if i - distance in devices]
    return lax.ppermute(block, axis, route)


def to_groups(k_ref, v_ref, out_ref, wide):
    for which, ref in enumerate((k_ref, v_ref)):
        wide[...] = ref[...].astype(jnp.float32)
        for g in range(wide.shape[1]):
            out_ref[g, which] = wide[:, g, :].astype(out_ref.dtype)


def from_groups(in_ref, k_ref, v_ref, wide):
    for which, ref in enumerate((k_ref, v_ref)):
        for g in range(wide.shape[1]):
            wide[:, g, :] = in_ref[g, which].astype(jnp.float32)
        ref[...] = wide[...].astype(ref.dtype)


def stage(q_hbm, g_hbm, q_ref, g_ref, sem):
    copies = [
        pltpu.make_async_copy(src, dst, sem.at[i])
        for i, (src, dst) in enumerate(((q_hbm, q_ref), (g_hbm, g_ref)))
    ]
    for copy in copies:
        copy.start()
    for copy in copies:
        copy.wait()


NT = (((1,), (1,)), ((), ()))
SPAN = (BACK + 1) * BLK
LOCAL = BLK_DEV * BLK
SPANS = [slice(o * BLK, (o + 1) * BLK) for o in range(BACK + 1)]


def scores_kernel(prev_ref, q_ref, g_ref, x0_ref, x1_ref, x2_ref,
                  y1_ref, y2_ref, d_ref, own_ref,
                  kk, vv, dk, dv, st_buf, dp_buf, p_buf, *, heads, rows):
    total_rows, head_size = q_ref.shape
    scale = 1.0 / math.sqrt(head_size)
    factor = scale * LOG2E
    f32 = jnp.float32
    low = kk.dtype
    chunks = total_rows // rows
    per_block = chunks // BLK_DEV
    far = BLK_DEV * LOCAL

    for i, ref in enumerate((x2_ref, x1_ref, x0_ref)):
        kk[i * LOCAL:(i + 1) * LOCAL] = ref[:, 0].reshape(LOCAL, head_size)
        vv[i * LOCAL:(i + 1) * LOCAL] = ref[:, 1].reshape(LOCAL, head_size)
    dk[...] = jnp.zeros_like(dk)
    dv[...] = jnp.zeros_like(dv)
    off = [
        [jnp.where(prev_ref[b] >= BACK - o, 0.0, OFF).astype(f32) for o in range(BACK)] + [None]
        for b in range(BLK_DEV)
    ]

    def place(c):
        base = c // per_block * BLK
        return slice(base, base + SPAN), slice(c * rows, (c + 1) * rows)

    def score_part(c):
        window, here = place(c)
        st_buf[c % 2] = lax.dot_general(kk[window], q_ref[here], NT, preferred_element_type=f32)

    def dprob_part(c):
        window, here = place(c)
        dp_buf[c % 2] = lax.dot_general(vv[window], g_ref[here], NT, preferred_element_type=f32)

    def exp_part(c):
        st = st_buf.at[c % 2]
        shut = off[c // per_block]
        key = lax.broadcasted_iota(jnp.int32, (BLK, rows), 0) * heads
        row = lax.broadcasted_iota(jnp.int32, (BLK, rows), 1) + c % per_block * rows
        own = jnp.where(key <= row, st[SPANS[BACK]], -OFF)
        top = jnp.max(own, axis=0, keepdims=True)
        for o in range(BACK):
            top = jnp.maximum(top, jnp.max(st[SPANS[o]], axis=0, keepdims=True) - shut[o])
        shift = top * factor
        total = jnp.zeros((1, rows), f32)
        for o in range(BACK + 1):
            if o == BACK:
                e = jnp.exp2(own * factor - shift)
            else:
                e = jnp.exp2(st[SPANS[o]] * factor - (shift + shut[o]))
            total = total + jnp.sum(e, axis=0, keepdims=True)
            st[SPANS[o]] = e
        return 1.0 / total

    def near(c):
        return BACK - c // per_block

    def prob_part(c, inv):
        st, dp = st_buf.at[c % 2], dp_buf.at[c % 2]
        delta = jnp.zeros((1, rows), f32)
        for o in range(BACK + 1):
            p_low = (st[SPANS[o]] * inv).astype(low)
            if o < near(c):
                p_buf[c % 2, SPANS[o]] = p_low
            else:
                own_ref[c, SPANS[o - BACK + 1]] = p_low
            delta = delta + jnp.sum(p_low.astype(f32) * dp[SPANS[o]], axis=0, keepdims=True)
        return delta

    def dscore_part(c, inv, delta):
        st, dp = st_buf.at[c % 2], dp_buf.at[c % 2]
        for o in range(BACK + 1):
            ds = st[SPANS[o]] * inv * (dp[SPANS[o]] - delta) * scale
            d_ref[c, SPANS[o]] = ds.astype(low)

    def value_part(c):
        window, here = place(c)
        count = near(c) * BLK
        dv[window.start:far] += jnp.dot(p_buf[c % 2, :count], g_ref[here], preferred_element_type=f32)

    def key_part(c):
        window, here = place(c)
        count = near(c) * BLK
        dk[window.start:far] += jnp.dot(d_ref[c, :count], q_ref[here], preferred_element_type=f32)

    for c in range(-1, chunks + 1):
        first, inside, last = c + 1 < chunks, 0 <= c < chunks, c >= 1
        if first:
            score_part(c + 1)
        if inside:
            inv = exp_part(c)
        if last:
            value_part(c - 1)
        if first:
            dprob_part(c + 1)
        if inside:
            delta = prob_part(c, inv)
        if last:
            key_part(c - 1)
        if inside:
            dscore_part(c, inv, delta)
    for i, ref in enumerate((y2_ref, y1_ref)):
        k = dk[i * LOCAL:(i + 1) * LOCAL]
        v = dv[i * LOCAL:(i + 1) * LOCAL]
        ref[:, 0] = k.astype(low).reshape(ref.shape[0], -1, head_size)
        ref[:, 1] = v.astype(low).reshape(ref.shape[0], -1, head_size)


def finish_kernel(q_ref, g_ref, x0_ref, x1_ref, x2_ref, d_ref, own_ref,
                  dq_hbm, y0_ref, dq_all, kt, dk, dv, sem, *, rows, pieces):
    total_rows, head_size = q_ref.shape
    f32 = jnp.float32
    low = kt.dtype
    chunks = total_rows // rows
    per_block = chunks // BLK_DEV
    piece = total_rows // pieces
    per_piece = chunks // pieces

    def put(i):
        part = pl.ds(i * piece, piece)
        return pltpu.make_async_copy(dq_all.at[part], dq_hbm.at[part], sem.at[i])

    for i, ref in enumerate((x2_ref, x1_ref, x0_ref)):
        k = ref[:, 0].reshape(LOCAL, head_size)
        kt[:, i * LOCAL:(i + 1) * LOCAL] = k.astype(f32).T.astype(low)
    dk[...] = jnp.zeros_like(dk)
    dv[...] = jnp.zeros_like(dv)
    for c in range(chunks):
        block = c // per_block
        here = slice(c * rows, (c + 1) * rows)
        held = slice(0, (block + 1) * BLK)
        d_low = d_ref[c]
        dqt = jnp.dot(kt[:, block * BLK:block * BLK + SPAN], d_low, preferred_element_type=f32)
        dk[held] += jnp.dot(d_low[SPAN - held.stop:], q_ref[here], preferred_element_type=f32)
        dv[held] += jnp.dot(own_ref[c, LOCAL - held.stop:], g_ref[here], preferred_element_type=f32)
        dq_all[here] = dqt.T.astype(low)
        if (c + 1) % per_piece == 0:
            put(c // per_piece).start()
    y0_ref[:, 0] = dk[...].astype(low).reshape(y0_ref.shape[0], -1, head_size)
    y0_ref[:, 1] = dv[...].astype(low).reshape(y0_ref.shape[0], -1, head_size)
    for i in range(pieces):
        put(i).wait()


def staged(q, g):
    return pl.pallas_call(
        stage,
        out_shape=(jax.ShapeDtypeStruct(q.shape, q.dtype), jax.ShapeDtypeStruct(g.shape, g.dtype)),
        in_specs=[HBM, HBM],
        out_specs=(VMEM, VMEM),
        scratch_shapes=[pltpu.SemaphoreType.DMA((2,))],
        cost_estimate=pl.CostEstimate(flops=0, bytes_accessed=4 * q.size * 2, transcendentals=0),
        compiler_params=pltpu.CompilerParams(vmem_limit_bytes=8 << 20),
        name="stage",
    )(q, g)


def remote_grads(prev, q, g, x0, x1, x2, heads, rows):
    head_size = q.shape[1]
    keys = 3 * LOCAL
    chunks = q.shape[0] // rows
    low = q.dtype
    f32 = jnp.float32
    pairs = 2 * BACK + 2
    return pl.pallas_call(
        functools.partial(scores_kernel, heads=heads, rows=rows),
        out_shape=(
            jax.ShapeDtypeStruct(x0.shape, low),
            jax.ShapeDtypeStruct(x0.shape, low),
            jax.ShapeDtypeStruct((chunks, SPAN, rows), low),
            jax.ShapeDtypeStruct((chunks, LOCAL, rows), low),
        ),
        in_specs=[SMEM] + [VMEM] * 5,
        out_specs=(VMEM,) * 4,
        scratch_shapes=[
            pltpu.VMEM((keys, head_size), low),
            pltpu.VMEM((keys, head_size), low),
            pltpu.VMEM((2 * LOCAL, head_size), f32),
            pltpu.VMEM((2 * LOCAL, head_size), f32),
            pltpu.VMEM((2, SPAN, rows), f32),
            pltpu.VMEM((2, SPAN, rows), f32),
            pltpu.VMEM((2, BACK * BLK, rows), low),
        ],
        cost_estimate=pl.CostEstimate(
            flops=2 * 4 * SPAN * q.size, bytes_accessed=8 * q.size, transcendentals=SPAN * q.shape[0]
        ),
        compiler_params=pltpu.CompilerParams(vmem_limit_bytes=24 << 20),
        name="remote_grads",
    )(prev, q, g, x0, x1, x2)


def own_grads(q, g, x0, x1, x2, d_low, own, pieces=4):
    head_size = q.shape[1]
    rows = d_low.shape[2]
    low = q.dtype
    f32 = jnp.float32
    return pl.pallas_call(
        functools.partial(finish_kernel, rows=rows, pieces=pieces),
        out_shape=(jax.ShapeDtypeStruct(q.shape, low), jax.ShapeDtypeStruct(x0.shape, low)),
        in_specs=[VMEM] * 7,
        out_specs=(HBM, VMEM),
        scratch_shapes=[
            pltpu.VMEM(q.shape, low),
            pltpu.VMEM((head_size, 3 * LOCAL), low),
            pltpu.VMEM((LOCAL, head_size), f32),
            pltpu.VMEM((LOCAL, head_size), f32),
            pltpu.SemaphoreType.DMA((pieces,)),
        ],
        cost_estimate=pl.CostEstimate(
            flops=2 * 2 * SPAN * q.size, bytes_accessed=8 * q.size, transcendentals=0
        ),
        compiler_params=pltpu.CompilerParams(vmem_limit_bytes=16 << 20),
        name="own_grads",
    )(q, g, x0, x1, x2, d_low, own)


def local_grads(prev, q, g, x0, x1, x2, heads, rows=512):
    y1, y2, d_low, own = remote_grads(prev, q, g, x0, x1, x2, heads, rows)
    dq, y0 = own_grads(q, g, x0, x1, x2, d_low, own)
    return dq, y0, y1, y2


def on_device(queries, keys, values, output_gradient, doc_blocks):
    tok_count, heads, head_size = queries.shape
    tok_part, groups, _ = keys.shape
    low = queries.dtype
    packed = pl.pallas_call(
        to_groups,
        out_shape=jax.ShapeDtypeStruct((groups, 2, tok_part, head_size), low),
        in_specs=[VMEM, VMEM],
        out_specs=VMEM,
        scratch_shapes=[pltpu.VMEM(keys.shape, jnp.float32)],
        name="to_groups",
    )(keys, values)
    x0 = lax.all_to_all(packed, "tp", split_axis=0, concat_axis=0, tiled=True)
    x1 = passed_along(x0, "ctx", 1)
    x2 = passed_along(x0, "ctx", 2)
    docs = doc_blocks.shape[0]
    upto = jnp.arange(docs)[:, None] >= jnp.arange(docs)[None, :]
    ends = jnp.sum(jnp.where(upto, doc_blocks[None, :], 0), axis=1)
    mine = lax.axis_index("ctx") * BLK_DEV + jnp.arange(BLK_DEV, dtype=jnp.int32)
    start = jnp.max(jnp.where(ends[None, :] <= mine[:, None], ends[None, :], 0), axis=1)
    prev = (mine - start).astype(jnp.int32)
    q, g = staged(
        queries.reshape(tok_count * heads, head_size),
        output_gradient.reshape(tok_count * heads, head_size),
    )
    y1, y2, d_low, own = remote_grads(prev, q, g, x0, x1, x2, heads, 256)
    r2 = passed_along(y2, "ctx", -2)
    r1 = passed_along(y1, "ctx", -1)
    dq, y0 = own_grads(q, g, x0, x1, x2, d_low, own)
    f32 = jnp.float32
    summed = (y0.astype(f32) + r1.astype(f32) + r2.astype(f32)).astype(low)
    back = lax.all_to_all(summed, "tp", split_axis=0, concat_axis=0, tiled=True)
    key_gradient, value_gradient = pl.pallas_call(
        from_groups,
        out_shape=(
            jax.ShapeDtypeStruct(keys.shape, low),
            jax.ShapeDtypeStruct(values.shape, low),
        ),
        in_specs=[VMEM],
        out_specs=(VMEM, VMEM),
        scratch_shapes=[pltpu.VMEM(keys.shape, jnp.float32)],
        name="from_groups",
    )(back)
    return dq.reshape(queries.shape), key_gradient, value_gradient


def solution(mesh):
    return jax.shard_map(
        on_device,
        mesh=mesh,
        in_specs=(
            P("ctx", "tp", None),
            P(("ctx", "tp"), None, None),
            P(("ctx", "tp"), None, None),
            P("ctx", "tp", None),
            P(),
        ),
        out_specs=(
            P("ctx", "tp", None),
            P(("ctx", "tp"), None, None),
            P(("ctx", "tp"), None, None),
        ),
        check_vma=False,
    )
```

```python
import functools
import math

import jax
import jax.numpy as jnp
from jax import lax
from jax.experimental import pallas as pl
from jax.experimental.pallas import tpu as pltpu
from jax.sharding import PartitionSpec as P

BLK = 128
BLK_DEV = 2
BACK = 4
LOG2E = math.log2(math.e)
OFF = 1.0e30

VMEM = pl.BlockSpec(memory_space=pltpu.VMEM)
SMEM = pl.BlockSpec(memory_space=pltpu.SMEM)
HBM = pl.BlockSpec(memory_space=pltpu.HBM)


def passed_along(block, axis, distance):
    devices = range(lax.axis_size(axis))
    route = [(i - distance, i) for i in devices if i - distance in devices]
    return lax.ppermute(block, axis, route)


def to_groups(k_ref, v_ref, out_ref, wide):
    for which, ref in enumerate((k_ref, v_ref)):
        wide[...] = ref[...].astype(jnp.float32)
        for g in range(wide.shape[1]):
            out_ref[g, which] = wide[:, g, :].astype(out_ref.dtype)


def from_groups(in_ref, k_ref, v_ref, wide):
    for which, ref in enumerate((k_ref, v_ref)):
        for g in range(wide.shape[1]):
            wide[:, g, :] = in_ref[g, which].astype(jnp.float32)
        ref[...] = wide[...].astype(ref.dtype)


def stage(q_hbm, g_hbm, q_ref, g_ref, sem):
    copies = [
        pltpu.make_async_copy(src, dst, sem.at[i])
        for i, (src, dst) in enumerate(((q_hbm, q_ref), (g_hbm, g_ref)))
    ]
    for copy in copies:
        copy.start()
    for copy in copies:
        copy.wait()


NT = (((1,), (1,)), ((), ()))
SPAN = (BACK + 1) * BLK
LOCAL = BLK_DEV * BLK
SPANS = [slice(o * BLK, (o + 1) * BLK) for o in range(BACK + 1)]


def block_scores(st, factor):
    top = jnp.max(st, axis=0, keepdims=True) * factor
    e = jnp.exp2(st * factor - top)
    return e, top, jnp.sum(e, axis=0, keepdims=True)


def part_kernel(q_ref, g_ref, x_ref, e_ref, dp_ref, top_ref, sum_ref, st_buf, *, heads, rows, own):
    total_rows, head_size = q_ref.shape
    factor = LOG2E / math.sqrt(head_size)
    f32 = jnp.float32
    chunks = total_rows // rows
    per_block = chunks // BLK_DEV
    k = x_ref[:, 0].reshape(LOCAL, head_size)
    v = x_ref[:, 1].reshape(LOCAL, head_size)

    def count(c):
        return c // per_block + 1 if own else BLK_DEV

    def products(c):
        here, size = slice(c * rows, (c + 1) * rows), count(c) * BLK
        st_buf[c % 2, :size] = lax.dot_general(k[:size], q_ref[here], NT, preferred_element_type=f32)
        dp_ref[c, :size] = lax.dot_general(v[:size], g_ref[here], NT, preferred_element_type=f32)

    def exponentials(c):
        for j in range(count(c)):
            st = st_buf[c % 2, SPANS[j]]
            if own and j == c // per_block:
                key = lax.broadcasted_iota(jnp.int32, (BLK, rows), 0) * heads
                row = lax.broadcasted_iota(jnp.int32, (BLK, rows), 1) + c % per_block * rows
                st = jnp.where(key <= row, st, -OFF)
            e, top, total = block_scores(st, factor)
            e_ref[c, SPANS[j]] = e
            top_ref[c, j:j + 1] = top
            sum_ref[c, j:j + 1] = total

    products(0)
    for c in range(chunks):
        if c + 1 < chunks:
            products(c + 1)
        exponentials(c)


def scores_kernel(prev_ref, q_ref, g_ref, x2_ref, e0_ref, dp0_ref, top0_ref, sum0_ref,
                  e1_ref, dp1_ref, top1_ref, sum1_ref,
                  y1_ref, y2_ref, d_ref, own_ref,
                  dk, dv, st_buf, e_buf, dp_buf, p_buf, *, heads, rows):
    total_rows, head_size = q_ref.shape
    scale = 1.0 / math.sqrt(head_size)
    factor = scale * LOG2E
    f32 = jnp.float32
    low = q_ref.dtype
    chunks = total_rows // rows
    per_block = chunks // BLK_DEV
    far = BLK_DEV * LOCAL
    k = x2_ref[:, 0].reshape(LOCAL, head_size)
    v = x2_ref[:, 1].reshape(LOCAL, head_size)
    dk[...] = jnp.zeros_like(dk)
    dv[...] = jnp.zeros_like(dv)
    off = [
        [jnp.where(prev_ref[b] >= BACK - o, 0.0, OFF).astype(f32) for o in range(BACK)] + [None]
        for b in range(BLK_DEV)
    ]

    def away(c):
        return BACK - c // per_block

    def score_part(c):
        here, base = slice(c * rows, (c + 1) * rows), c // per_block * BLK
        st_buf[c % 2, base:] = lax.dot_general(k[base:], q_ref[here], NT, preferred_element_type=f32)

    def dprob_part(c):
        here, base = slice(c * rows, (c + 1) * rows), c // per_block * BLK
        dp_buf[c % 2, base:] = lax.dot_general(v[base:], g_ref[here], NT, preferred_element_type=f32)

    def parts(c):
        found = []
        for o in range(BACK + 1):
            place, j = divmod(c // per_block + o, BLK_DEV)
            if place == 0:
                found.append((e_buf.at[c % 2], dp_buf.at[c % 2], None, None, j))
            elif place == 1:
                found.append((e1_ref.at[c], dp1_ref.at[c], top1_ref, sum1_ref, j))
            else:
                found.append((e0_ref.at[c], dp0_ref.at[c], top0_ref, sum0_ref, j))
        return found

    def exp_part(c):
        tops, sums = [], []
        for _, _, top_ref, sum_ref, j in parts(c):
            if top_ref is None:
                e, top, total = block_scores(st_buf[c % 2, SPANS[j]], factor)
                e_buf[c % 2, SPANS[j]] = e
            else:
                top, total = top_ref[c, j:j + 1], sum_ref[c, j:j + 1]
            tops.append(top)
            sums.append(total)
        shut = off[c // per_block]
        tops = [t if s is None else t - s for t, s in zip(tops, shut)]
        top = functools.reduce(jnp.maximum, tops)
        shares = [jnp.exp2(t - top) for t in tops]
        inv = 1.0 / functools.reduce(jnp.add, [a * b for a, b in zip(shares, sums)])
        return [share * inv for share in shares]

    def prob_part(c, shares):
        delta = jnp.zeros((1, rows), f32)
        for o, (e, dp, _, _, j) in enumerate(parts(c)):
            p_low = (e[SPANS[j]] * shares[o]).astype(low)
            if o < away(c):
                p_buf[c % 2, SPANS[o]] = p_low
            else:
                own_ref[c, SPANS[o - BACK + 1]] = p_low
            delta = delta + jnp.sum(p_low.astype(f32) * dp[SPANS[j]], axis=0, keepdims=True)
        return delta

    def dscore_part(c, shares, delta):
        for o, (e, dp, _, _, j) in enumerate(parts(c)):
            ds = e[SPANS[j]] * shares[o] * (dp[SPANS[j]] - delta) * scale
            d_ref[c, SPANS[o]] = ds.astype(low)

    def value_part(c):
        here, base, size = slice(c * rows, (c + 1) * rows), c // per_block * BLK, away(c) * BLK
        dv[base:far] += jnp.dot(p_buf[c % 2, :size], g_ref[here], preferred_element_type=f32)

    def key_part(c):
        here, base, size = slice(c * rows, (c + 1) * rows), c // per_block * BLK, away(c) * BLK
        dk[base:far] += jnp.dot(d_ref[c, :size], q_ref[here], preferred_element_type=f32)

    for c in range(-1, chunks + 1):
        first, inside, last = c + 1 < chunks, 0 <= c < chunks, c >= 1
        if first:
            score_part(c + 1)
        if inside:
            shares = exp_part(c)
        if last:
            value_part(c - 1)
        if first:
            dprob_part(c + 1)
        if inside:
            delta = prob_part(c, shares)
        if last:
            key_part(c - 1)
        if inside:
            dscore_part(c, shares, delta)
    for i, ref in enumerate((y2_ref, y1_ref)):
        dk_part = dk[i * LOCAL:(i + 1) * LOCAL]
        dv_part = dv[i * LOCAL:(i + 1) * LOCAL]
        ref[:, 0] = dk_part.astype(low).reshape(ref.shape[0], -1, head_size)
        ref[:, 1] = dv_part.astype(low).reshape(ref.shape[0], -1, head_size)


def finish_kernel(q_ref, g_ref, x0_ref, x1_ref, x2_ref, d_ref, own_ref,
                  dq_hbm, y0_ref, dq_all, kt, dk, dv, sem, *, rows, pieces):
    total_rows, head_size = q_ref.shape
    f32 = jnp.float32
    low = kt.dtype
    chunks = total_rows // rows
    per_block = chunks // BLK_DEV
    piece = total_rows // pieces
    per_piece = chunks // pieces

    def put(i):
        part = pl.ds(i * piece, piece)
        return pltpu.make_async_copy(dq_all.at[part], dq_hbm.at[part], sem.at[i])

    for i, ref in enumerate((x2_ref, x1_ref, x0_ref)):
        k = ref[:, 0].reshape(LOCAL, head_size)
        kt[:, i * LOCAL:(i + 1) * LOCAL] = k.astype(f32).T.astype(low)
    dk[...] = jnp.zeros_like(dk)
    dv[...] = jnp.zeros_like(dv)
    for c in range(chunks):
        block = c // per_block
        here = slice(c * rows, (c + 1) * rows)
        held = slice(0, (block + 1) * BLK)
        d_low = d_ref[c]
        dqt = jnp.dot(kt[:, block * BLK:block * BLK + SPAN], d_low, preferred_element_type=f32)
        dk[held] += jnp.dot(d_low[SPAN - held.stop:], q_ref[here], preferred_element_type=f32)
        dv[held] += jnp.dot(own_ref[c, LOCAL - held.stop:], g_ref[here], preferred_element_type=f32)
        dq_all[here] = dqt.T.astype(low)
        if (c + 1) % per_piece == 0:
            put(c // per_piece).start()
    y0_ref[:, 0] = dk[...].astype(low).reshape(y0_ref.shape[0], -1, head_size)
    y0_ref[:, 1] = dv[...].astype(low).reshape(y0_ref.shape[0], -1, head_size)
    for i in range(pieces):
        put(i).wait()


def staged(q, g):
    return pl.pallas_call(
        stage,
        out_shape=(jax.ShapeDtypeStruct(q.shape, q.dtype), jax.ShapeDtypeStruct(g.shape, g.dtype)),
        in_specs=[HBM, HBM],
        out_specs=(VMEM, VMEM),
        scratch_shapes=[pltpu.SemaphoreType.DMA((2,))],
        cost_estimate=pl.CostEstimate(flops=0, bytes_accessed=4 * q.size * 2, transcendentals=0),
        compiler_params=pltpu.CompilerParams(vmem_limit_bytes=8 << 20),
        name="stage",
    )(q, g)


def part_scores(q, g, x, heads, rows, own):
    chunks = q.shape[0] // rows
    f32 = jnp.float32
    big = jax.ShapeDtypeStruct((chunks, LOCAL, rows), f32)
    small = jax.ShapeDtypeStruct((chunks, 8, rows), f32)
    return pl.pallas_call(
        functools.partial(part_kernel, heads=heads, rows=rows, own=own),
        out_shape=(big, big, small, small),
        in_specs=[VMEM] * 3,
        out_specs=(VMEM,) * 4,
        scratch_shapes=[pltpu.VMEM((2, LOCAL, rows), f32)],
        cost_estimate=pl.CostEstimate(
            flops=2 * 2 * LOCAL * q.size, bytes_accessed=4 * q.size, transcendentals=LOCAL * q.shape[0]
        ),
        compiler_params=pltpu.CompilerParams(vmem_limit_bytes=4 << 20),
        name="own_scores" if own else "near_scores",
    )(q, g, x)


def remote_grads(prev, q, g, x2, own, near, heads, rows):
    head_size = q.shape[1]
    chunks = q.shape[0] // rows
    low = q.dtype
    f32 = jnp.float32
    return pl.pallas_call(
        functools.partial(scores_kernel, heads=heads, rows=rows),
        out_shape=(
            jax.ShapeDtypeStruct(x2.shape, low),
            jax.ShapeDtypeStruct(x2.shape, low),
            jax.ShapeDtypeStruct((chunks, SPAN, rows), low),
            jax.ShapeDtypeStruct((chunks, LOCAL, rows), low),
        ),
        in_specs=[SMEM] + [VMEM] * 11,
        out_specs=(VMEM,) * 4,
        scratch_shapes=[
            pltpu.VMEM((2 * LOCAL, head_size), f32),
            pltpu.VMEM((2 * LOCAL, head_size), f32),
            pltpu.VMEM((2, LOCAL, rows), f32),
            pltpu.VMEM((2, LOCAL, rows), f32),
            pltpu.VMEM((2, LOCAL, rows), f32),
            pltpu.VMEM((2, BACK * BLK, rows), low),
        ],
        cost_estimate=pl.CostEstimate(
            flops=2 * 4 * SPAN * q.size, bytes_accessed=8 * q.size, transcendentals=SPAN * q.shape[0]
        ),
        compiler_params=pltpu.CompilerParams(vmem_limit_bytes=10 << 20),
        name="remote_grads",
    )(prev, q, g, x2, *own, *near)


def own_grads(q, g, x0, x1, x2, d_low, own, pieces=4):
    head_size = q.shape[1]
    rows = d_low.shape[2]
    low = q.dtype
    f32 = jnp.float32
    return pl.pallas_call(
        functools.partial(finish_kernel, rows=rows, pieces=pieces),
        out_shape=(jax.ShapeDtypeStruct(q.shape, low), jax.ShapeDtypeStruct(x0.shape, low)),
        in_specs=[VMEM] * 7,
        out_specs=(HBM, VMEM),
        scratch_shapes=[
            pltpu.VMEM(q.shape, low),
            pltpu.VMEM((head_size, 3 * LOCAL), low),
            pltpu.VMEM((LOCAL, head_size), f32),
            pltpu.VMEM((LOCAL, head_size), f32),
            pltpu.SemaphoreType.DMA((pieces,)),
        ],
        cost_estimate=pl.CostEstimate(
            flops=2 * 2 * SPAN * q.size, bytes_accessed=8 * q.size, transcendentals=0
        ),
        compiler_params=pltpu.CompilerParams(vmem_limit_bytes=16 << 20),
        name="own_grads",
    )(q, g, x0, x1, x2, d_low, own)


def local_grads(prev, q, g, x0, x1, x2, heads, rows=256):
    own = part_scores(q, g, x0, heads, rows, True)
    near = part_scores(q, g, x1, heads, rows, False)
    y1, y2, d_low, p_own = remote_grads(prev, q, g, x2, own, near, heads, rows)
    dq, y0 = own_grads(q, g, x0, x1, x2, d_low, p_own)
    return dq, y0, y1, y2


def on_device(queries, keys, values, output_gradient, doc_blocks):
    tok_count, heads, head_size = queries.shape
    tok_part, groups, _ = keys.shape
    low = queries.dtype
    packed = pl.pallas_call(
        to_groups,
        out_shape=jax.ShapeDtypeStruct((groups, 2, tok_part, head_size), low),
        in_specs=[VMEM, VMEM],
        out_specs=VMEM,
        scratch_shapes=[pltpu.VMEM(keys.shape, jnp.float32)],
        name="to_groups",
    )(keys, values)
    x0 = lax.all_to_all(packed, "tp", split_axis=0, concat_axis=0, tiled=True)
    x1 = passed_along(x0, "ctx", 1)
    x2 = passed_along(x0, "ctx", 2)
    docs = doc_blocks.shape[0]
    upto = jnp.arange(docs)[:, None] >= jnp.arange(docs)[None, :]
    ends = jnp.sum(jnp.where(upto, doc_blocks[None, :], 0), axis=1)
    mine = lax.axis_index("ctx") * BLK_DEV + jnp.arange(BLK_DEV, dtype=jnp.int32)
    start = jnp.max(jnp.where(ends[None, :] <= mine[:, None], ends[None, :], 0), axis=1)
    prev = (mine - start).astype(jnp.int32)
    q, g = staged(
        queries.reshape(tok_count * heads, head_size),
        output_gradient.reshape(tok_count * heads, head_size),
    )
    rows = 256
    own = part_scores(q, g, x0, heads, rows, True)
    near = part_scores(q, g, x1, heads, rows, False)
    y1, y2, d_low, p_own = remote_grads(prev, q, g, x2, own, near, heads, rows)
    r2 = passed_along(y2, "ctx", -2)
    r1 = passed_along(y1, "ctx", -1)
    dq, y0 = own_grads(q, g, x0, x1, x2, d_low, p_own)
    f32 = jnp.float32
    summed = (y0.astype(f32) + r1.astype(f32) + r2.astype(f32)).astype(low)
    back = lax.all_to_all(summed, "tp", split_axis=0, concat_axis=0, tiled=True)
    key_gradient, value_gradient = pl.pallas_call(
        from_groups,
        out_shape=(
            jax.ShapeDtypeStruct(keys.shape, low),
            jax.ShapeDtypeStruct(values.shape, low),
        ),
        in_specs=[VMEM],
        out_specs=(VMEM, VMEM),
        scratch_shapes=[pltpu.VMEM(keys.shape, jnp.float32)],
        name="from_groups",
    )(back)
    return dq.reshape(queries.shape), key_gradient, value_gradient


def solution(mesh):
    return jax.shard_map(
        on_device,
        mesh=mesh,
        in_specs=(
            P("ctx", "tp", None),
            P(("ctx", "tp"), None, None),
            P(("ctx", "tp"), None, None),
            P("ctx", "tp", None),
            P(),
        ),
        out_specs=(
            P("ctx", "tp", None),
            P(("ctx", "tp"), None, None),
            P(("ctx", "tp"), None, None),
        ),
        check_vma=False,
    )
```

```python
import functools
import math

import jax
import jax.numpy as jnp
from jax import lax
from jax.experimental import pallas as pl
from jax.experimental.pallas import tpu as pltpu
from jax.sharding import PartitionSpec as P


BLK = 128
BLK_DEV = 2
BACK = 4
LOG2E = math.log2(math.e)
OFF = 1.0e30

VMEM = pl.BlockSpec(memory_space=pltpu.VMEM)
SMEM = pl.BlockSpec(memory_space=pltpu.SMEM)
HBM = pl.BlockSpec(memory_space=pltpu.HBM)


def passed_along(block, axis, distance):
    devices = range(lax.axis_size(axis))
    route = [(i - distance, i) for i in devices if i - distance in devices]
    return lax.ppermute(block, axis, route)


def to_groups(k_ref, v_ref, out_ref, wide):
    for which, ref in enumerate((k_ref, v_ref)):
        wide[...] = ref[...].astype(jnp.float32)
        for g in range(wide.shape[1]):
            out_ref[g, which] = wide[:, g, :].astype(out_ref.dtype)


def from_groups(in_ref, k_ref, v_ref, wide):
    for which, ref in enumerate((k_ref, v_ref)):
        for g in range(wide.shape[1]):
            wide[:, g, :] = in_ref[g, which].astype(jnp.float32)
        ref[...] = wide[...].astype(ref.dtype)


def stage(q_hbm, g_hbm, q_ref, g_ref, sem):
    copies = [
        pltpu.make_async_copy(src, dst, sem.at[i])
        for i, (src, dst) in enumerate(((q_hbm, q_ref), (g_hbm, g_ref)))
    ]
    for copy in copies:
        copy.start()
    for copy in copies:
        copy.wait()


NT = (((1,), (1,)), ((), ()))
SPAN = (BACK + 1) * BLK
LOCAL = BLK_DEV * BLK
SPANS = [slice(o * BLK, (o + 1) * BLK) for o in range(BACK + 1)]


def block_scores(st, factor):
    top = jnp.max(st, axis=0, keepdims=True) * factor
    e = jnp.exp2(st * factor - top)
    return e, top, jnp.sum(e, axis=0, keepdims=True)


def part_kernel(q_ref, g_ref, x_ref, e_ref, dp_ref, top_ref, sum_ref, st_buf, *, heads, rows, own):
    total_rows, head_size = q_ref.shape
    factor = LOG2E / math.sqrt(head_size)
    f32 = jnp.float32
    chunks = total_rows // rows
    per_block = chunks // BLK_DEV
    k = x_ref[:, 0].reshape(LOCAL, head_size)
    v = x_ref[:, 1].reshape(LOCAL, head_size)

    def count(c):
        return c // per_block + 1 if own else BLK_DEV

    def products(c):
        here, size = slice(c * rows, (c + 1) * rows), count(c) * BLK
        st_buf[c % 2, :size] = lax.dot_general(k[:size], q_ref[here], NT, preferred_element_type=f32)
        dp_ref[c, :size] = lax.dot_general(v[:size], g_ref[here], NT, preferred_element_type=f32)

    def exponentials(c):
        for j in range(count(c)):
            st = st_buf[c % 2, SPANS[j]]
            if own and j == c // per_block:
                key = lax.broadcasted_iota(jnp.int32, (BLK, rows), 0) * heads
                row = lax.broadcasted_iota(jnp.int32, (BLK, rows), 1) + c % per_block * rows
                st = jnp.where(key <= row, st, -OFF)
            e, top, total = block_scores(st, factor)
            e_ref[c, SPANS[j]] = e
            top_ref[c, j:j + 1] = top
            sum_ref[c, j:j + 1] = total

    products(0)
    for c in range(chunks):
        if c + 1 < chunks:
            products(c + 1)
        exponentials(c)


def scores_kernel(prev_ref, q_ref, g_ref, x2_ref, e0_ref, dp0_ref, top0_ref, sum0_ref,
                  e1_ref, dp1_ref, top1_ref, sum1_ref,
                  y1_ref, y2_ref, d_ref, own_ref,
                  dk, dv, st_buf, e_buf, dp_buf, p_buf, *, heads, rows):
    total_rows, head_size = q_ref.shape
    scale = 1.0 / math.sqrt(head_size)
    factor = scale * LOG2E
    f32 = jnp.float32
    low = q_ref.dtype
    chunks = total_rows // rows
    per_block = chunks // BLK_DEV
    far = BLK_DEV * LOCAL
    k = x2_ref[:, 0].reshape(LOCAL, head_size)
    v = x2_ref[:, 1].reshape(LOCAL, head_size)
    dk[...] = jnp.zeros_like(dk)
    dv[...] = jnp.zeros_like(dv)
    off = [
        [jnp.where(prev_ref[b] >= BACK - o, 0.0, OFF).astype(f32) for o in range(BACK)] + [None]
        for b in range(BLK_DEV)
    ]

    def away(c):
        return BACK - c // per_block

    def score_part(c):
        here, base = slice(c * rows, (c + 1) * rows), c // per_block * BLK
        st_buf[c % 2, base:] = lax.dot_general(k[base:], q_ref[here], NT, preferred_element_type=f32)

    def dprob_part(c):
        here, base = slice(c * rows, (c + 1) * rows), c // per_block * BLK
        dp_buf[c % 2, base:] = lax.dot_general(v[base:], g_ref[here], NT, preferred_element_type=f32)

    def parts(c):
        found = []
        for o in range(BACK + 1):
            place, j = divmod(c // per_block + o, BLK_DEV)
            if place == 0:
                found.append((e_buf.at[c % 2], dp_buf.at[c % 2], None, None, j))
            elif place == 1:
                found.append((e1_ref.at[c], dp1_ref.at[c], top1_ref, sum1_ref, j))
            else:
                found.append((e0_ref.at[c], dp0_ref.at[c], top0_ref, sum0_ref, j))
        return found

    def exp_part(c):
        tops, sums = [], []
        for _, _, top_ref, sum_ref, j in parts(c):
            if top_ref is None:
                e, top, total = block_scores(st_buf[c % 2, SPANS[j]], factor)
                e_buf[c % 2, SPANS[j]] = e
            else:
                top, total = top_ref[c, j:j + 1], sum_ref[c, j:j + 1]
            tops.append(top)
            sums.append(total)
        shut = off[c // per_block]
        tops = [t if s is None else t - s for t, s in zip(tops, shut)]
        top = functools.reduce(jnp.maximum, tops)
        shares = [jnp.exp2(t - top) for t in tops]
        inv = 1.0 / functools.reduce(jnp.add, [a * b for a, b in zip(shares, sums)])
        return [share * inv for share in shares]

    def prob_part(c, shares):
        delta = jnp.zeros((1, rows), f32)
        for o, (e, dp, _, _, j) in enumerate(parts(c)):
            p_low = (e[SPANS[j]] * shares[o]).astype(low)
            if o < away(c):
                p_buf[c % 2, SPANS[o]] = p_low
            else:
                own_ref[c, SPANS[o - BACK + 1]] = p_low
            delta = delta + jnp.sum(p_low.astype(f32) * dp[SPANS[j]], axis=0, keepdims=True)
        return delta

    def dscore_part(c, shares, delta):
        for o, (e, dp, _, _, j) in enumerate(parts(c)):
            ds = e[SPANS[j]] * shares[o] * (dp[SPANS[j]] - delta) * scale
            d_ref[c, SPANS[o]] = ds.astype(low)

    def value_part(c):
        here, base, size = slice(c * rows, (c + 1) * rows), c // per_block * BLK, away(c) * BLK
        dv[base:far] += jnp.dot(p_buf[c % 2, :size], g_ref[here], preferred_element_type=f32)

    def key_part(c):
        here, base, size = slice(c * rows, (c + 1) * rows), c // per_block * BLK, away(c) * BLK
        dk[base:far] += jnp.dot(d_ref[c, :size], q_ref[here], preferred_element_type=f32)

    for c in range(-1, chunks + 1):
        first, inside, last = c + 1 < chunks, 0 <= c < chunks, c >= 1
        if first:
            score_part(c + 1)
        if inside:
            shares = exp_part(c)
        if last:
            value_part(c - 1)
        if first:
            dprob_part(c + 1)
        if inside:
            delta = prob_part(c, shares)
        if last:
            key_part(c - 1)
        if inside:
            dscore_part(c, shares, delta)
    for i, ref in enumerate((y2_ref, y1_ref)):
        dk_part = dk[i * LOCAL:(i + 1) * LOCAL]
        dv_part = dv[i * LOCAL:(i + 1) * LOCAL]
        ref[:, 0] = dk_part.astype(low).reshape(ref.shape[0], -1, head_size)
        ref[:, 1] = dv_part.astype(low).reshape(ref.shape[0], -1, head_size)


def finish_kernel(q_ref, g_ref, x0_ref, x1_ref, x2_ref, d_ref, own_ref,
                  dq_hbm, y0_ref, dq_all, kt, dk, dv, sem, *, rows, pieces):
    total_rows, head_size = q_ref.shape
    f32 = jnp.float32
    low = kt.dtype
    chunks = total_rows // rows
    per_block = chunks // BLK_DEV
    piece = total_rows // pieces
    per_piece = chunks // pieces

    def put(i):
        part = pl.ds(i * piece, piece)
        return pltpu.make_async_copy(dq_all.at[part], dq_hbm.at[part], sem.at[i])

    for i, ref in enumerate((x2_ref, x1_ref, x0_ref)):
        k = ref[:, 0].reshape(LOCAL, head_size)
        kt[:, i * LOCAL:(i + 1) * LOCAL] = k.astype(f32).T.astype(low)
    dk[...] = jnp.zeros_like(dk)
    dv[...] = jnp.zeros_like(dv)
    for c in range(chunks):
        block = c // per_block
        here = slice(c * rows, (c + 1) * rows)
        held = slice(0, (block + 1) * BLK)
        d_low = d_ref[c]
        dqt = jnp.dot(kt[:, block * BLK:block * BLK + SPAN], d_low, preferred_element_type=f32)
        dk[held] += jnp.dot(d_low[SPAN - held.stop:], q_ref[here], preferred_element_type=f32)
        dv[held] += jnp.dot(own_ref[c, LOCAL - held.stop:], g_ref[here], preferred_element_type=f32)
        dq_all[here] = dqt.T.astype(low)
        if (c + 1) % per_piece == 0:
            put(c // per_piece).start()
    y0_ref[:, 0] = dk[...].astype(low).reshape(y0_ref.shape[0], -1, head_size)
    y0_ref[:, 1] = dv[...].astype(low).reshape(y0_ref.shape[0], -1, head_size)
    for i in range(pieces):
        put(i).wait()


def staged(q, g):
    return pl.pallas_call(
        stage,
        out_shape=(jax.ShapeDtypeStruct(q.shape, q.dtype), jax.ShapeDtypeStruct(g.shape, g.dtype)),
        in_specs=[HBM, HBM],
        out_specs=(VMEM, VMEM),
        scratch_shapes=[pltpu.SemaphoreType.DMA((2,))],
        cost_estimate=pl.CostEstimate(flops=0, bytes_accessed=4 * q.size * 2, transcendentals=0),
        compiler_params=pltpu.CompilerParams(vmem_limit_bytes=8 << 20),
        name="stage",
    )(q, g)


def part_scores(q, g, x, heads, rows, own):
    chunks = q.shape[0] // rows
    f32 = jnp.float32
    big = jax.ShapeDtypeStruct((chunks, LOCAL, rows), f32)
    small = jax.ShapeDtypeStruct((chunks, 8, rows), f32)
    return pl.pallas_call(
        functools.partial(part_kernel, heads=heads, rows=rows, own=own),
        out_shape=(big, big, small, small),
        in_specs=[VMEM] * 3,
        out_specs=(VMEM,) * 4,
        scratch_shapes=[pltpu.VMEM((2, LOCAL, rows), f32)],
        cost_estimate=pl.CostEstimate(
            flops=2 * 2 * LOCAL * q.size, bytes_accessed=4 * q.size, transcendentals=LOCAL * q.shape[0]
        ),
        compiler_params=pltpu.CompilerParams(vmem_limit_bytes=4 << 20),
        name="own_scores" if own else "near_scores",
    )(q, g, x)


def remote_grads(prev, q, g, x2, own, near, heads, rows):
    head_size = q.shape[1]
    chunks = q.shape[0] // rows
    low = q.dtype
    f32 = jnp.float32
    return pl.pallas_call(
        functools.partial(scores_kernel, heads=heads, rows=rows),
        out_shape=(
            jax.ShapeDtypeStruct(x2.shape, low),
            jax.ShapeDtypeStruct(x2.shape, low),
            jax.ShapeDtypeStruct((chunks, SPAN, rows), low),
            jax.ShapeDtypeStruct((chunks, LOCAL, rows), low),
        ),
        in_specs=[SMEM] + [VMEM] * 11,
        out_specs=(VMEM,) * 4,
        scratch_shapes=[
            pltpu.VMEM((2 * LOCAL, head_size), f32),
            pltpu.VMEM((2 * LOCAL, head_size), f32),
            pltpu.VMEM((2, LOCAL, rows), f32),
            pltpu.VMEM((2, LOCAL, rows), f32),
            pltpu.VMEM((2, LOCAL, rows), f32),
            pltpu.VMEM((2, BACK * BLK, rows), low),
        ],
        cost_estimate=pl.CostEstimate(
            flops=2 * 4 * SPAN * q.size, bytes_accessed=8 * q.size, transcendentals=SPAN * q.shape[0]
        ),
        compiler_params=pltpu.CompilerParams(vmem_limit_bytes=10 << 20),
        name="remote_grads",
    )(prev, q, g, x2, *own, *near)


def own_grads(q, g, x0, x1, x2, d_low, own, pieces=4):
    head_size = q.shape[1]
    rows = d_low.shape[2]
    low = q.dtype
    f32 = jnp.float32
    return pl.pallas_call(
        functools.partial(finish_kernel, rows=rows, pieces=pieces),
        out_shape=(jax.ShapeDtypeStruct(q.shape, low), jax.ShapeDtypeStruct(x0.shape, low)),
        in_specs=[VMEM] * 7,
        out_specs=(HBM, VMEM),
        scratch_shapes=[
            pltpu.VMEM(q.shape, low),
            pltpu.VMEM((head_size, 3 * LOCAL), low),
            pltpu.VMEM((LOCAL, head_size), f32),
            pltpu.VMEM((LOCAL, head_size), f32),
            pltpu.SemaphoreType.DMA((pieces,)),
        ],
        cost_estimate=pl.CostEstimate(
            flops=2 * 2 * SPAN * q.size, bytes_accessed=8 * q.size, transcendentals=0
        ),
        compiler_params=pltpu.CompilerParams(vmem_limit_bytes=16 << 20),
        name="own_grads",
    )(q, g, x0, x1, x2, d_low, own)


def on_device(queries, keys, values, output_gradient, doc_blocks):
    tok_count, heads, head_size = queries.shape
    tok_part, groups, _ = keys.shape
    low = queries.dtype
    packed = pl.pallas_call(
        to_groups,
        out_shape=jax.ShapeDtypeStruct((groups, 2, tok_part, head_size), low),
        in_specs=[VMEM, VMEM],
        out_specs=VMEM,
        scratch_shapes=[pltpu.VMEM(keys.shape, jnp.float32)],
        name="to_groups",
    )(keys, values)
    x0 = lax.all_to_all(packed, "tp", split_axis=0, concat_axis=0, tiled=True)
    x1 = passed_along(x0, "ctx", 1)
    x2 = passed_along(x0, "ctx", 2)
    docs = doc_blocks.shape[0]
    upto = jnp.arange(docs)[:, None] >= jnp.arange(docs)[None, :]
    ends = jnp.sum(jnp.where(upto, doc_blocks[None, :], 0), axis=1)
    mine = lax.axis_index("ctx") * BLK_DEV + jnp.arange(BLK_DEV, dtype=jnp.int32)
    start = jnp.max(jnp.where(ends[None, :] <= mine[:, None], ends[None, :], 0), axis=1)
    prev = (mine - start).astype(jnp.int32)
    q, g = staged(
        queries.reshape(tok_count * heads, head_size),
        output_gradient.reshape(tok_count * heads, head_size),
    )
    rows = 256
    own = part_scores(q, g, x0, heads, rows, True)
    near = part_scores(q, g, x1, heads, rows, False)
    y1, y2, d_low, p_own = remote_grads(prev, q, g, x2, own, near, heads, rows)
    r2 = passed_along(y2, "ctx", -2)
    r1 = passed_along(y1, "ctx", -1)
    dq, y0 = own_grads(q, g, x0, x1, x2, d_low, p_own)
    f32 = jnp.float32
    summed = (y0.astype(f32) + r1.astype(f32) + r2.astype(f32)).astype(low)
    back = lax.all_to_all(summed, "tp", split_axis=0, concat_axis=0, tiled=True)
    key_gradient, value_gradient = pl.pallas_call(
        from_groups,
        out_shape=(
            jax.ShapeDtypeStruct(keys.shape, low),
            jax.ShapeDtypeStruct(values.shape, low),
        ),
        in_specs=[VMEM],
        out_specs=(VMEM, VMEM),
        scratch_shapes=[pltpu.VMEM(keys.shape, jnp.float32)],
        name="from_groups",
    )(back)
    return dq.reshape(queries.shape), key_gradient, value_gradient


def solution(mesh):
    return jax.shard_map(
        on_device,
        mesh=mesh,
        in_specs=(
            P("ctx", "tp", None),
            P(("ctx", "tp"), None, None),
            P(("ctx", "tp"), None, None),
            P("ctx", "tp", None),
            P(),
        ),
        out_specs=(
            P("ctx", "tp", None),
            P(("ctx", "tp"), None, None),
            P(("ctx", "tp"), None, None),
        ),
        check_vma=False,
    )
```
